32 devices in a mesh: section: 2 (over x), peer: 16 (over z, y, core).
Axes of the slice: x: 2, y: 2, z: 4, core: 2. Of those that a mesh axis runs over, the one named last changes fastest.
Arguments:
- rows_in: bfloat16 [2, 2048, 5120], P('section', 'peer')
- returned: bfloat16 [2, 2048, 5120], P('section', 'peer'), may hold values from -6 to 6
- norm_gain: bfloat16 [2, 5120], P('section'), may hold values from 0.099609375 to 1.8984375
- adapter_down: bfloat16 [2, 5120, 16], P('section'), may hold values from -0.078125 to 0.078125
- adapter_up: bfloat16 [2, 16, 5120], P('section'), may hold values from -1.5 to 1.5
- wiring: int32 [2, 16], P('section', 'peer'), may hold values from 0 to 15, as said below
Outputs:
- forward_rows: bfloat16 [2, 2048, 5120], P('section', 'peer')
- grad_down: float32 [2, 5120, 16], P('section')
- grad_up: float32 [2, 16, 5120], P('section')
The draws below stay inside these ranges and needn't reach their ends.
Inputs may be any that keep to these rules, and one draw needn't show every extreme that they name: For each section s there is a mask m below 16 with wiring[s, p] = p XOR m for every peer p; each section's entries are a permutation of the peers.
All inputs are finite; a program needn't handle non-finite values.
Results may differ from the reference program's by a relative error of at most 0.0058.
Values may be sent and summed in bfloat16 or wider, within the bound.
No kernel may reach another device: no remote copies, remote signals or barrier semaphores. Data moves between devices by JAX's collectives and lax.ppermute only.
A program may use at most 64 MiB of HBM per device.

```python
import math
import jax
import jax.numpy as jnp
from jax import lax

D = 5120
R = 16
ROWS = 128
BITS = 4
REACH = 16
SECTIONS = 2
TOTAL_ROWS = 2048
N_PEER = 16


def draw_rows_in(key, part):
    base_key, row_key, col_key = jax.random.split(key, 3)
    shape = (SECTIONS, TOTAL_ROWS, D)
    base = jax.random.normal(base_key, shape, jnp.float32)
    row_scale = jnp.exp(jax.random.uniform(row_key, (SECTIONS, TOTAL_ROWS, 1), jnp.float32, math.log(0.01), math.log(0.1)))
    col_scale = jnp.exp(jax.random.uniform(col_key, (1, 1, D), jnp.float32, math.log(0.5), math.log(2.0)))
    return jnp.clip(base * row_scale * col_scale, -24.0, 24.0).astype(jnp.bfloat16)


def draw_wiring(key, part):
    section_ids = jnp.arange(SECTIONS, dtype=jnp.int32)
    section_masks = jax.random.randint(key, (SECTIONS,), 0, REACH, dtype=jnp.int32)
    section_masks = jnp.bitwise_or(section_masks, jnp.left_shift(jnp.ones((SECTIONS,), jnp.int32), section_ids % BITS))
    peer_ids = jnp.arange(N_PEER, dtype=jnp.int32)
    return jnp.bitwise_xor(peer_ids[None, :], section_masks[:, None])


def block_levels(own_key, shape, cuts, low, top_value):
    gain, own = 1.0, jax.random.fold_in(own_key, 6)
    for position, parts in cuts:
        heights = jnp.exp(jax.random.uniform(jax.random.fold_in(own, position), (parts,), jnp.float32, low / len(cuts), top_value / len(cuts)))
        gain = gain * jnp.repeat(heights, shape[position] // parts).reshape([-1 if axis == position else 1 for axis in range(len(shape))])
    return gain


def bell_draw(stream_key, shape, scale, limit, cuts=(), held_as=jnp.bfloat16):
    loudness = block_levels(stream_key, shape, cuts, -0.22, 0.18) if cuts else 1.0
    drawn = jax.random.normal(stream_key, shape, jnp.float32) * scale * loudness
    return jnp.minimum(jnp.maximum(drawn, -limit), limit).astype(held_as)


def setup_inputs(seed: int = 0) -> dict:
    arg_keys = jax.random.split(jax.random.key(seed), 7)
    rows_in = draw_rows_in(jax.random.fold_in(arg_keys[6], 71), 0)
    returned = bell_draw(arg_keys[1], (SECTIONS, TOTAL_ROWS, D), 1.0, 6.0, ((0, 2), (1, 16)))
    norm_gain = jnp.clip(1.0 + 0.18 * jax.random.normal(arg_keys[2], (SECTIONS, D), jnp.float32), 0.099609375, 1.8984375).astype(jnp.bfloat16)
    adapter_down = bell_draw(arg_keys[3], (SECTIONS, D, R), D ** -0.5, 0.078125, ((0, 2),))
    adapter_up = bell_draw(arg_keys[4], (SECTIONS, R, D), R ** -0.5, 1.5, ((0, 2),))
    wiring = draw_wiring(jax.random.fold_in(arg_keys[6], 71), 0)
    return {"rows_in": rows_in, "returned": returned, "norm_gain": norm_gain, "adapter_down": adapter_down, "adapter_up": adapter_up, "wiring": wiring}


EPSILON = 1e-05

def section_pass(operands):
    inputs, upstream, gain_row, down_matrix, up_matrix = operands
    inputs_f = inputs.astype(jnp.float32)
    mean_square = lax.optimization_barrier(jnp.mean(inputs_f * inputs_f, axis=-1, keepdims=True))
    normed = (inputs_f * lax.rsqrt(mean_square + EPSILON) * gain_row.astype(jnp.float32)).astype(jnp.bfloat16)
    latent = jnp.einsum('prd,dk->prk', normed.astype(jnp.float32), down_matrix.astype(jnp.float32)).astype(jnp.bfloat16)
    outputs = (inputs_f + jnp.einsum('prk,kd->prd', latent.astype(jnp.float32), up_matrix.astype(jnp.float32))).astype(jnp.bfloat16)
    grad_up_sum = jnp.einsum('prk,prd->kd', latent.astype(jnp.float32), upstream.astype(jnp.float32))
    latent_grad = jnp.einsum('prd,kd->prk', upstream.astype(jnp.float32), up_matrix.astype(jnp.float32)).astype(jnp.bfloat16)
    grad_down_sum = jnp.einsum('prd,prk->dk', normed.astype(jnp.float32), latent_grad.astype(jnp.float32))
    return (outputs, grad_down_sum / N_PEER, grad_up_sum / N_PEER)

def reference(rows_in, returned, norm_gain, adapter_down, adapter_up, wiring):
    inputs = rows_in.reshape(SECTIONS, N_PEER, ROWS, D)
    gradient_rows = returned.reshape(SECTIONS, N_PEER, ROWS, D)
    next_section = ((jnp.arange(SECTIONS, dtype=jnp.int32) + 1) % SECTIONS)[:, None]
    upstream = gradient_rows[next_section, wiring]
    outputs, grad_down, grad_up = lax.map(section_pass, (inputs, upstream, norm_gain, adapter_down, adapter_up))
    moved = jnp.zeros_like(outputs).at[next_section, wiring].set(outputs)
    return (moved.reshape(SECTIONS, TOTAL_ROWS, D), grad_down, grad_up)
```

```python
import jax
import jax.numpy as jnp
from jax import lax
from jax.sharding import PartitionSpec as P

BITS = 4
EPSILON = 1e-05
HALVINGS = 2
PIECES = ((0, 48), (48, 40), (88, 40))
ROUTES = ((3, 2, 1, 0, "x"), (1, 3, 2, 0, "x"), ("x", 1, 0, 2, 3))


def from_partner(value, mask):
    count = lax.axis_size("peer")
    return lax.ppermute(value, "peer", [(source, source ^ mask) for source in range(count)])


def passed_along(value, by):
    count = lax.axis_size("section")
    return lax.ppermute(value, "section", [(i, (i + by) % count) for i in range(count)])


def bit_set(mask, bit):
    return jnp.bitwise_and(jnp.right_shift(mask, bit), 1) == 1


def routed(value, mask):
    def branch(fixed):
        return lambda v: from_partner(v, fixed) if fixed else v

    return lax.switch(mask, [branch(fixed) for fixed in range(2**BITS)], value)


def walk(piece, route, own_mask, prior_mask):
    mask = own_mask
    for hop in route:
        if hop == "x":
            piece = passed_along(piece, 1)
            mask = prior_mask
        else:
            piece = jnp.where(bit_set(mask, hop), from_partner(piece, 2**hop), piece)
    return piece


def summed_over_peers(terms):
    peers = lax.axis_size("peer")
    position = lax.axis_index("peer")
    bits = peers.bit_length() - 1
    halvings = min(HALVINGS, bits)
    part = terms
    for bit in range(halvings):
        width = part.shape[-1] // 2
        side = jnp.bitwise_and(jnp.right_shift(position, bit), 1)
        kept = lax.dynamic_slice_in_dim(part, side * width, width, 2)
        given = lax.dynamic_slice_in_dim(part, (1 - side) * width, width, 2)
        part = kept + from_partner(given.astype(jnp.bfloat16), 2**bit).astype(jnp.float32)
    for bit in range(halvings, bits):
        mine = part.astype(jnp.bfloat16)
        part = mine.astype(jnp.float32) + from_partner(mine, 2**bit).astype(jnp.float32)
    part = part.astype(jnp.bfloat16)
    part = jnp.stack([part[0], passed_along(part[1], -1)])
    for bit in reversed(range(halvings)):
        other = from_partner(part, 2**bit)
        lower = bit_set(position, bit)
        part = jnp.concatenate(
            [jnp.where(lower, other, part), jnp.where(lower, part, other)], axis=2
        )
    return part


def shards(rows_in, returned, norm_gain, adapter_down, adapter_up, wiring):
    peers = lax.axis_size("peer")
    rows = rows_in[0]
    upstream = returned[0]
    up_matrix = adapter_up[0]
    own_mask = jnp.bitwise_xor(wiring[0, 0], lax.axis_index("peer"))
    prior_mask = passed_along(own_mask, 1)
    up_prior = passed_along(up_matrix, 1)

    moved = [
        walk(rows[at : at + size], route, own_mask, prior_mask)
        for (at, size), route in zip(PIECES, ROUTES)
    ]

    inputs_f = rows.astype(jnp.float32)
    mean_square = jnp.mean(inputs_f * inputs_f, axis=-1, keepdims=True)
    normed = (
        inputs_f * lax.rsqrt(mean_square + EPSILON) * norm_gain[0].astype(jnp.float32)
    ).astype(jnp.bfloat16)
    latent = lax.dot_general(
        adapter_down[0], normed, (((0,), (1,)), ((), ())), preferred_element_type=jnp.float32
    ).astype(jnp.bfloat16)
    grad_prior = lax.dot_general(
        up_prior, upstream, (((1,), (1,)), ((), ())), preferred_element_type=jnp.float32
    ).astype(jnp.bfloat16)
    small = routed(jnp.stack([latent, passed_along(grad_prior, -1)]), own_mask)
    latent_prior = passed_along(small[0], 1)
    term_down = jnp.dot(small[1], normed, preferred_element_type=jnp.float32)
    term_prior = jnp.dot(latent_prior, upstream, preferred_element_type=jnp.float32)
    sums = summed_over_peers(jnp.stack([term_down, term_prior])).astype(jnp.float32) / peers

    added = lax.dot_general(
        latent_prior, up_prior, (((0,), (0,)), ((), ())), preferred_element_type=jnp.float32
    )
    onward = jnp.concatenate(
        [
            (piece.astype(jnp.float32) + added[at : at + size]).astype(jnp.bfloat16)
            for (at, size), piece in zip(PIECES, moved)
        ]
    )
    return onward[None], sums[0].T[None], sums[1][None]


def solution(mesh):
    in_specs = (
        P("section", "peer", None),
        P("section", "peer", None),
        P("section", None),
        P("section", None, None),
        P("section", None, None),
        P("section", "peer"),
    )
    out_specs = (P("section", "peer", None), P("section", None, None), P("section", None, None))
    return jax.shard_map(shards, mesh=mesh, in_specs=in_specs, out_specs=out_specs, check_vma=False)
```

```python
import jax
import jax.numpy as jnp
from jax import lax
from jax.sharding import PartitionSpec as P


BITS = 4
EPSILON = 1e-05
HALVINGS = 2


def from_partner(value, mask):
    count = lax.axis_size("peer")
    return lax.ppermute(value, "peer", [(source, source ^ mask) for source in range(count)])


def passed_along(value, by):
    count = lax.axis_size("section")
    return lax.ppermute(value, "section", [(i, (i + by) % count) for i in range(count)])


def bit_set(mask, bit):
    return jnp.bitwise_and(jnp.right_shift(mask, bit), 1) == 1


def routed(value, mask):
    def branch(fixed):
        return lambda v: from_partner(v, fixed) if fixed else v

    return lax.switch(mask, [branch(fixed) for fixed in range(2**BITS)], value)


def hops(piece, bits, mask):
    for bit in bits:
        moved = from_partner(piece, 2**bit)
        piece = jnp.where(bit_set(mask, bit), moved, piece)
    return piece


def halves(piece):
    middle = piece.shape[0] // 2
    return piece[:middle], piece[middle:]


def summed_over_peers(terms):
    peers = lax.axis_size("peer")
    position = lax.axis_index("peer")
    bits = peers.bit_length() - 1
    halvings = min(HALVINGS, bits)
    part = terms
    for bit in range(halvings):
        width = part.shape[-1] // 2
        side = jnp.bitwise_and(jnp.right_shift(position, bit), 1)
        kept = lax.dynamic_slice_in_dim(part, side * width, width, 2)
        given = lax.dynamic_slice_in_dim(part, (1 - side) * width, width, 2)
        part = kept + from_partner(given.astype(jnp.bfloat16), 2**bit).astype(jnp.float32)
    for bit in range(halvings, bits):
        mine = part.astype(jnp.bfloat16)
        part = mine.astype(jnp.float32) + from_partner(mine, 2**bit).astype(jnp.float32)
    part = part.astype(jnp.bfloat16)
    part = jnp.stack([part[0], passed_along(part[1], -1)])
    for bit in reversed(range(halvings)):
        other = from_partner(part, 2**bit)
        lower = bit_set(position, bit)
        part = jnp.concatenate(
            [jnp.where(lower, other, part), jnp.where(lower, part, other)], axis=2
        )
    return part


def body(rows_in, returned, norm_gain, adapter_down, adapter_up, wiring):
    peers = lax.axis_size("peer")
    rows = rows_in[0]
    upstream = returned[0]
    up_matrix = adapter_up[0]
    own_mask = jnp.bitwise_xor(wiring[0, 0], lax.axis_index("peer"))
    up_prior = passed_along(up_matrix, 1)

    inputs_f = rows.astype(jnp.float32)
    mean_square = jnp.mean(inputs_f * inputs_f, axis=-1, keepdims=True)
    normed = (
        inputs_f * lax.rsqrt(mean_square + EPSILON) * norm_gain[0].astype(jnp.float32)
    ).astype(jnp.bfloat16)
    latent = lax.dot_general(
        adapter_down[0], normed, (((0,), (1,)), ((), ())), preferred_element_type=jnp.float32
    ).astype(jnp.bfloat16)
    grad_prior = lax.dot_general(
        up_prior, upstream, (((1,), (1,)), ((), ())), preferred_element_type=jnp.float32
    ).astype(jnp.bfloat16)
    small = routed(jnp.stack([latent, passed_along(grad_prior, -1)]), own_mask)
    mask_rows = jnp.full_like(small[0], own_mask.astype(jnp.bfloat16))
    prior = passed_along(jnp.stack([small[0], mask_rows]), 1)
    latent_prior = prior[0]
    prior_mask = prior[1, 0, 0].astype(jnp.int32)
    early, late = halves(rows)
    first, second = halves(early)
    early = jnp.concatenate([hops(first, (3, 2), own_mask), hops(second, (2, 3), own_mask)])
    early = passed_along(hops(early, (1, 0), own_mask), 1)
    late = passed_along(hops(late, (1,), own_mask), 1)
    first, second = halves(hops(late, (0,), prior_mask))
    moved = [early, hops(first, (3, 2), prior_mask), hops(second, (2, 3), prior_mask)]
    term_down = jnp.dot(small[1], normed, preferred_element_type=jnp.float32)
    term_prior = jnp.dot(latent_prior, upstream, preferred_element_type=jnp.float32)
    sums = summed_over_peers(jnp.stack([term_down, term_prior])).astype(jnp.float32) / peers

    added = lax.dot_general(
        latent_prior, up_prior, (((0,), (0,)), ((), ())), preferred_element_type=jnp.float32
    )
    onward = (jnp.concatenate(moved).astype(jnp.float32) + added).astype(jnp.bfloat16)
    return onward[None], sums[0].T[None], sums[1][None]


def solution(mesh):
    in_specs = (
        P("section", "peer", None),
        P("section", "peer", None),
        P("section", None),
        P("section", None, None),
        P("section", None, None),
        P("section", "peer"),
    )
    out_specs = (P("section", "peer", None), P("section", None, None), P("section", None, None))
    return jax.shard_map(body, mesh=mesh, in_specs=in_specs, out_specs=out_specs, check_vma=False)
```
